256 devices in a mesh: region: 32 (over x, y, core), helper: 8 (over z).
Axes of the slice: x: 4, y: 4, z: 8, core: 2. Of those that a mesh axis runs over, the one named last changes fastest.
Arguments:
- bricks: bfloat16 [32, 262144], P(None, ('region', 'helper')), may hold values from -6 to 6
- positions: float32 [3, 512, 4096], P(None, 'region', 'helper'), may hold values from 0 to 7
- spacing: float32 [512, 4096], P('region', 'helper'), may hold values from 0.002 to 0.02
- brick_ids: int32 [512, 32], P('region', 'helper'), may hold values from 0 to 15, as said below
- region_rank: int32 [4096, 32], P('helper'), may hold values from 0 to 31, each once within a row
- target: float32 [3, 4096], P(None, 'helper'), may hold values from 0 to 1
- in_weight: bfloat16 [64, 32], replicated, may hold values from -1 to 1
- in_bias: float32 [64], replicated, may hold values from -3 to 3
- out_weight: bfloat16 [4, 64], replicated, may hold values from -0.75 to 0.75
- out_bias: float32 [4], replicated, may hold values from -3 to 3
Outputs:
- colour: float32 [3, 4096], P(None, 'helper')
- brick_grad: float32 [32, 262144], P(None, ('region', 'helper'))
The draws below stay inside these ranges and needn't reach their ends.
Inputs may be any that keep to these rules, and one draw needn't show every extreme that they name: `brick_ids`: index of a brick among the 16 bricks of the region that holds the tile; bricks h * 2 to (h + 1) * 2 - 1 belong to index h of helper. Of the tiles of one device (columns j * 4 to (j + 1) * 4 - 1 and rows r * 16 to (r + 1) * 16 - 1), at most 16 name bricks of one index of helper; in every region some index of helper is named by exactly 16 tiles of every device of that region. `region_rank`: each row is a permutation: every region has a distinct place along every ray.
All inputs are finite; a program needn't handle non-finite values.
Results may differ from the reference program's by a relative error of at most 0.0021.
Values may be sent and summed in bfloat16 or wider, within the bound.
No kernel may reach another device: no remote copies, remote signals or barrier semaphores. Data moves between devices by JAX's collectives and lax.ppermute only.
A program may use at most 64 MiB of HBM per device.

```python
import math
import jax
import jax.numpy as jnp
from jax import lax

C = 32
HID = 64
SEG = 16
BRICK_DEV = 2
RAY_DEV = 512
RAYS = 4096
TOTAL_VOX = 262144
N_REGION = 32
N_HELPER = 8


def draw_brick_ids(key, part):
    tiles = SEG * (RAY_DEV // 128)
    capacity = 2 * tiles // N_HELPER
    slots = N_HELPER * capacity

    def draw_device(region, source):
        region_key = jax.random.fold_in(jax.random.fold_in(key, 17), region)
        busiest = jax.random.randint(region_key, (), 0, N_HELPER)
        device_key = jax.random.fold_in(jax.random.fold_in(region_key, 29), source)
        key_order, key_shuffle, key_within = jax.random.split(device_key, 3)
        slot_ids = jnp.arange(slots, dtype=jnp.int32)
        ordering = jax.random.permutation(key_order, slots).astype(jnp.int32)
        scores = jnp.where(slot_ids // capacity == busiest, slot_ids - slots, ordering)
        chosen = jnp.argsort(scores, stable=True)[:tiles].astype(jnp.int32)
        shuffle = jax.random.permutation(key_shuffle, tiles).astype(jnp.int32)
        chosen = chosen[shuffle]
        holder_of = (chosen // capacity).astype(jnp.int32)
        within = jax.random.randint(key_within, (tiles,), 0, BRICK_DEV).astype(jnp.int32)
        return (holder_of * BRICK_DEV + within).reshape(SEG, RAY_DEV // 128)

    def draw_region(region):

        def draw_source(source):
            return draw_device(region, source)
        return jax.vmap(draw_source)(jnp.arange(N_HELPER, dtype=jnp.int32))
    grid = jax.vmap(draw_region)(jnp.arange(N_REGION, dtype=jnp.int32))
    return grid.transpose(0, 2, 1, 3).reshape(N_REGION * SEG, RAYS // 128).astype(jnp.int32)


def level_of(key, shape, cuts, least, high):
    def one(dim, parts):
        draws = jax.random.uniform(jax.random.fold_in(jax.random.fold_in(key, 6), dim), (parts,), jnp.float32, least / len(cuts), high / len(cuts))
        return jnp.repeat(jnp.exp(draws), shape[dim] // parts).reshape((-1,) + (1,) * (len(shape) - dim - 1))

    factor_of = one(*cuts[0])
    for cut in cuts[1:]:
        factor_of = factor_of * one(*cut)
    return factor_of


def normal_values(stream_key, dims, deviation, reach, cuts=(), kind=jnp.bfloat16):
    array = deviation * jax.random.normal(stream_key, dims, jnp.float32)
    if cuts:
        array = array * level_of(stream_key, dims, cuts, -0.22, 0.18)
    return jnp.clip(array, -reach, reach).astype(kind)


def setup_inputs(seed: int = 0) -> dict:
    splits = jax.random.split(jax.random.key(seed), 11)
    return {
        "bricks": normal_values(splits[0], (C, TOTAL_VOX), 1.0, 6.0, ((1, 256),)),
        "positions": jnp.clip(7.0 * jax.random.uniform(splits[1], (3, N_REGION * SEG, RAYS), jnp.float32) ** level_of(splits[1], (3, N_REGION * SEG, RAYS), ((1, 32), (2, 8)), -0.2, 0.2), 0.0, 7.0),
        "spacing": jnp.clip(jnp.exp(math.log(0.02) - 2.30258502 * jax.random.uniform(splits[2], (N_REGION * SEG, RAYS), jnp.float32) ** level_of(splits[2], (N_REGION * SEG, RAYS), ((0, 32), (1, 8)), -0.2, 0.2)), 0.002, 0.02),
        "brick_ids": draw_brick_ids(jax.random.fold_in(splits[10], 71), 0),
        "region_rank": jax.vmap(lambda own: jax.random.permutation(own, N_REGION))(jax.random.split(splits[4], RAYS)).reshape((RAYS, N_REGION)).astype(jnp.int32),
        "target": jnp.clip(1.0 * jax.random.uniform(splits[5], (3, RAYS), jnp.float32) ** level_of(splits[5], (3, RAYS), ((1, 8),), -0.2, 0.2), 0.0, 1.0),
        "in_weight": normal_values(splits[6], (HID, C), C ** -0.5, 1.0),
        "in_bias": normal_values(splits[7], (HID,), 0.5, 3.0, (), jnp.float32),
        "out_weight": normal_values(splits[8], (4, HID), HID ** -0.5, 0.75),
        "out_bias": normal_values(splits[9], (4,), 0.5, 3.0, (), jnp.float32),
    }


def corners(positions, tile_bricks):
    lower = jnp.clip(jnp.floor(positions), 0.0, 6.0)
    fraction = positions - lower
    cell_index = lower.astype(jnp.int32)
    brick_base = jnp.repeat(tile_bricks, 128, axis=1).astype(jnp.int32) * 512
    listing = []
    for corner_x in (0, 1):
        for corner_y in (0, 1):
            for corner_z in (0, 1):
                lookup = brick_base + (cell_index[0] + corner_x) * 64 + (cell_index[1] + corner_y) * 8 + (cell_index[2] + corner_z)
                factor_x = fraction[0] if corner_x else 1.0 - fraction[0]
                factor_y = fraction[1] if corner_y else 1.0 - fraction[1]
                factor_z = fraction[2] if corner_z else 1.0 - fraction[2]
                listing.append((lookup, factor_x * factor_y * factor_z))
    return listing


def decode(table, positions, tile_bricks, in_weight, in_bias, out_weight, out_bias):
    channels = table.shape[0]
    samples, rays_here = positions.shape[1], positions.shape[2]
    listing = corners(positions, tile_bricks)
    feature = jnp.zeros((channels, samples, rays_here), jnp.float32)
    for lookup, corner_weight in listing:
        feature = feature + jnp.take(table, lookup, axis=1).astype(jnp.float32) * corner_weight[None]
    feature_flat = feature.astype(jnp.bfloat16).reshape(channels, -1)
    hidden_in = jnp.dot(in_weight, feature_flat, preferred_element_type=jnp.float32) + in_bias[:, None]
    hidden = jax.nn.silu(hidden_in).astype(jnp.bfloat16)
    decoded = jnp.dot(out_weight, hidden, preferred_element_type=jnp.float32) + out_bias[:, None]
    decoded = decoded.reshape(4, samples, rays_here)
    return decoded, (listing, hidden_in)


def render(decoded, spacing):
    density = jax.nn.softplus(decoded[0])
    radiance = jax.nn.sigmoid(decoded[1:])
    thickness = density * spacing
    optical = jnp.cumsum(thickness, axis=0)
    entering = jnp.exp(-(optical - thickness))
    weight = entering * (1.0 - jnp.exp(-thickness))
    segment_col = jnp.sum(weight[None] * radiance, axis=1)
    log_trans = -optical[-1]
    return log_trans, segment_col, (radiance, thickness, entering, weight)


def render_back(decoded, render_stash, grad_col, grad_log, spacing):
    radiance, thickness, entering, weight = render_stash
    mixing = jnp.sum(grad_col[:, None, :] * radiance, axis=0)
    leaving = entering * jnp.exp(-thickness)
    weighted = weight * mixing
    behind = jnp.sum(weighted, axis=0, keepdims=True) - jnp.cumsum(weighted, axis=0)
    grad_thick = leaving * mixing - behind - grad_log[None, :]
    grad_density = grad_thick * spacing * jax.nn.sigmoid(decoded[0])
    grad_radiance = weight[None] * grad_col[:, None, :] * radiance * (1.0 - radiance)
    return jnp.concatenate([grad_density[None], grad_radiance], 0)


def decode_back(decode_stash, grad_decoded, in_weight, out_weight, table_shape):
    listing, hidden_in = decode_stash
    channels = in_weight.shape[1]
    samples, rays_here = grad_decoded.shape[1], grad_decoded.shape[2]
    grad_hidden = jnp.dot(out_weight.astype(jnp.float32).T, grad_decoded.reshape(4, -1), precision=lax.Precision.HIGHEST)
    logistic = jax.nn.sigmoid(hidden_in)
    grad_in = (grad_hidden * logistic * (1.0 + hidden_in * (1.0 - logistic))).astype(jnp.bfloat16)
    grad_feature = jnp.dot(in_weight.T, grad_in, preferred_element_type=jnp.float32)
    grad_feature = grad_feature.reshape(channels, samples, rays_here)
    grad_table = jnp.zeros(table_shape, jnp.float32)
    for lookup, corner_weight in listing:
        grad_table = grad_table.at[:, lookup.reshape(-1)].add((grad_feature * corner_weight[None]).reshape(channels, -1))
    return grad_table


def compose(segment_data, ranking):
    ordering = jnp.argsort(ranking, axis=1).T.astype(jnp.int32)
    sorted_seg = jnp.take_along_axis(segment_data, jnp.broadcast_to(ordering[:, None, :], segment_data.shape), axis=0)
    optical = jnp.cumsum(sorted_seg[:, 0], axis=0)
    fading_sorted = jnp.exp(optical - sorted_seg[:, 0])
    contrib = fading_sorted[:, None, :] * sorted_seg[:, 1:]
    running = jnp.cumsum(contrib, axis=0)
    front_sorted = running - contrib
    colour = running[-1]
    position = ranking.T.astype(jnp.int32)
    fading = jnp.take_along_axis(fading_sorted, position, axis=0)
    in_front = jnp.take_along_axis(front_sorted, jnp.broadcast_to(position[:, None, :], front_sorted.shape), axis=0)
    return colour, fading, in_front


def reference(bricks, positions, spacing, brick_ids, region_rank, target, in_weight, in_bias, out_weight, out_bias):
    channels = bricks.shape[0]
    per_region = bricks.shape[1] // N_REGION
    table_all = bricks.reshape(channels, N_REGION, per_region).transpose(1, 0, 2)
    positions_all = positions.reshape(3, N_REGION, SEG, RAYS).transpose(1, 0, 2, 3)
    spacing_all = spacing.reshape(N_REGION, SEG, RAYS)
    tile_all = brick_ids.reshape(N_REGION, SEG, RAYS // 128)

    def forward_one(inputs_one):
        table, place_xyz, space, tiles = inputs_one
        decoded, decode_stash = decode(table, place_xyz, tiles, in_weight, in_bias, out_weight, out_bias)
        log_trans, segment_col, render_stash = render(decoded, space)
        return jnp.concatenate([log_trans[None], segment_col], 0)

    segment_data = lax.map(forward_one, (table_all, positions_all, spacing_all, tile_all))
    colour, fading, in_front = compose(segment_data, region_rank)
    residual = colour - target

    def backward_one(inputs_one):
        table, place_xyz, space, tiles, fading_one, front_one = inputs_one
        decoded, decode_stash = decode(table, place_xyz, tiles, in_weight, in_bias, out_weight, out_bias)
        log_trans, segment_col, render_stash = render(decoded, space)
        grad_col = fading_one[None] * residual
        grad_log = jnp.sum(residual * (colour - front_one - fading_one[None] * segment_col), axis=0)
        grad_decoded = render_back(decoded, render_stash, grad_col, grad_log, space)
        return decode_back(decode_stash, grad_decoded, in_weight, out_weight, table.shape)

    gradients = lax.map(backward_one, (table_all, positions_all, spacing_all, tile_all, fading, in_front))
    brick_grad = gradients.transpose(1, 0, 2).reshape(channels, -1)
    return colour, brick_grad
```

```python
import functools

import jax
import jax.numpy as jnp
from jax import lax
from jax.experimental import pallas as pl
from jax.experimental.pallas import tpu as pltpu
from jax.sharding import PartitionSpec as P

F32 = jnp.float32
BF16 = jnp.bfloat16


def axis_weights(places, tile):
    grid = lax.broadcasted_iota(jnp.int32, (8, 128), 0).astype(F32)
    return [
        jnp.maximum(1.0 - jnp.abs(places[tile, d : d + 1, :] - grid), 0.0) for d in range(3)
    ]


def plane_weights(wy, wz):
    wyz = (wy[:, None, :] * wz[None, :, :]).reshape(64, 128)
    high = wyz.astype(BF16)
    low = (wyz - high.astype(F32)).astype(BF16)
    return jnp.concatenate([high, low], axis=0)


def forward_kernel(
    ids, table, pos, spc, in_w, in_b, out_w, out_b, seg, feat, dec, places, planes, heads, optical
):
    samples, rays = spc.shape
    tiles = rays // 128
    bricks = planes.shape[0]

    for s in range(samples):
        for j in range(tiles):
            for d in range(3):
                places[s * tiles + j, d : d + 1, :] = pos[d, s : s + 1, j * 128 : (j + 1) * 128]

    def spread(b, carry):
        brick = table[b // 2, :, pl.ds(pl.multiple_of((b % 2) * 512, 512), 512)]
        for x in range(8):
            part = brick[:, x * 64 : (x + 1) * 64]
            planes[b, x * 32 : (x + 1) * 32, :] = jnp.concatenate([part, part], axis=1)
        return carry

    lax.fori_loop(0, bricks, spread, 0)

    def sample(s, carry):
        parts = []
        for j in range(tiles):
            wx, wy, wz = axis_weights(places, s * tiles + j)
            sums = jnp.dot(planes[ids[s, j]], plane_weights(wy, wz), preferred_element_type=F32)
            sums = sums.reshape(8, 32, 128) * wx[:, None, :]
            parts.append(jnp.sum(sums, axis=0).astype(BF16))
        feature = jnp.concatenate(parts, axis=1)
        feat[s] = feature
        hidden_in = jnp.dot(in_w[...], feature, preferred_element_type=F32) + in_b[...]
        hidden = (hidden_in * jax.nn.sigmoid(hidden_in)).astype(BF16)
        decoded = jnp.dot(out_w[...], hidden, preferred_element_type=F32) + out_b[...]
        heads[s] = decoded
        return carry

    lax.fori_loop(0, samples, sample, 0)

    for s in range(samples):
        for c in range(4):
            dec[c, s : s + 1, :] = heads[s, c : c + 1, :]

    raw = dec[0]
    density = jnp.maximum(raw, 0.0) + jnp.log1p(jnp.exp(-jnp.abs(raw)))
    thickness = density * spc[...]
    total = jnp.zeros((1, rays), F32)
    for s in range(samples):
        total = total + thickness[s : s + 1, :]
        optical[s : s + 1, :] = total
    entering = jnp.exp(thickness - optical[...])
    weight = entering * (1.0 - jnp.exp(-thickness))
    rows = [-total]
    for c in range(1, 4):
        rows.append(jnp.sum(weight * jax.nn.sigmoid(dec[c]), axis=0, keepdims=True))
    own = jnp.concatenate(
        [rows[c][:, j * 128 : (j + 1) * 128] for j in range(tiles) for c in range(4)], axis=0
    )
    seg[...] = jnp.broadcast_to(own[None], seg.shape)


def backward_kernel(
    ids,
    region,
    segs,
    rank,
    target,
    dec,
    feat,
    places,
    spc,
    in_w,
    in_b,
    out_w3,
    colour,
    contrib,
    total,
    back,
    grads,
    heads,
    scan,
):
    samples, rays = spc.shape
    tiles = rays // 128
    regions = rank.shape[0]
    bricks = total.shape[0]
    stride = segs.shape[0] // regions

    for b in range(bricks):
        total[b] = jnp.zeros(total.shape[1:], F32)

    for j in range(tiles):
        lanes = slice(j * 128, (j + 1) * 128)
        logs = segs[pl.ds(j * 4, regions, stride), :]
        order = rank[:, lanes]
        before = jnp.zeros((regions, 128), F32)
        for i in range(regions):
            log_i = segs[i * stride + j * 4 : i * stride + j * 4 + 1, :]
            before = before + jnp.where(rank[i : i + 1, lanes] < order, log_i, 0.0)
        fading = jnp.exp(before)
        row = lax.broadcasted_iota(jnp.int32, (regions, 128), 0)
        order_own = jnp.sum(jnp.where(row == region[0], order, 0), axis=0, keepdims=True)
        fading_own = jnp.exp(
            jnp.sum(jnp.where(order < order_own, logs, 0.0), axis=0, keepdims=True)
        )
        log_grad = jnp.zeros((1, 128), F32)
        for c in range(3):
            part = fading * segs[pl.ds(j * 4 + c + 1, regions, stride), :]
            seen = jnp.sum(part, axis=0, keepdims=True)
            behind = jnp.sum(jnp.where(order > order_own, part, 0.0), axis=0, keepdims=True)
            colour[c : c + 1, lanes] = seen
            residual = seen - target[c : c + 1, lanes]
            log_grad = log_grad + residual * behind
            back[c + 1 : c + 2, lanes] = fading_own * residual
        back[0:1, lanes] = log_grad

    raw = dec[0]
    thin = jnp.exp(-jnp.abs(raw))
    density = jnp.maximum(raw, 0.0) + jnp.log1p(thin)
    thickness = density * spc[...]
    run = jnp.zeros((1, rays), F32)
    for s in range(samples):
        scan[s : s + 1, :] = run
        run = run + thickness[s : s + 1, :]
    entering = jnp.exp(-scan[...])
    through = jnp.exp(-thickness)
    weight = entering * (1.0 - through)
    mixing = jnp.zeros((samples, rays), F32)
    for c in range(1, 4):
        radiance = jax.nn.sigmoid(dec[c])
        grad_col = back[c : c + 1, :]
        mixing = mixing + grad_col * radiance
        grads[c] = weight * grad_col * radiance * (1.0 - radiance)
    weighted = weight * mixing
    run = jnp.zeros((1, rays), F32)
    for s in reversed(range(samples)):
        scan[s : s + 1, :] = run
        run = run + weighted[s : s + 1, :]
    grad_thick = entering * through * mixing - scan[...] - back[0:1, :]
    grads[0] = grad_thick * spc[...] * jax.nn.sigmoid(raw)

    for s in range(samples):
        for c in range(4):
            heads[s, c : c + 1, :] = grads[c, s : s + 1, :]

    def sample(s, carry):
        grad = heads[s]
        high = grad.astype(BF16).astype(F32)
        rest = grad - high
        middle = rest.astype(BF16).astype(F32)
        low = rest - middle
        split = jnp.concatenate([high, middle, low, jnp.zeros_like(low)], axis=0).astype(BF16)
        grad_hidden = jnp.dot(out_w3[...], split, preferred_element_type=F32)
        hidden_in = jnp.dot(in_w[...], feat[s], preferred_element_type=F32) + in_b[...]
        logistic = jax.nn.sigmoid(hidden_in)
        slope = logistic * (1.0 + hidden_in * (1.0 - logistic))
        grad_in = (grad_hidden * slope).astype(BF16)
        grad_feature = lax.dot_general(
            in_w[...], grad_in, (((0,), (0,)), ((), ())), preferred_element_type=F32
        )
        for j in range(tiles):
            lanes = slice(j * 128, (j + 1) * 128)
            wx, wy, wz = axis_weights(places, s * tiles + j)
            spread = (wx[:, None, :] * grad_feature[None, :, lanes]).reshape(256, 128)
            total[ids[s, j]] += lax.dot_general(
                spread.astype(BF16),
                plane_weights(wy, wz),
                (((1,), (1,)), ((), ())),
                preferred_element_type=F32,
            )
        return carry

    lax.fori_loop(0, samples, sample, 0)

    first = lax.broadcasted_iota(jnp.int32, (32, 128), 1) < 64

    def gather(h, carry):
        for w in range(2):
            b = h * 2 + w
            for p in range(4):
                even = total[b, p * 64 : p * 64 + 32, :]
                odd = total[b, p * 64 + 32 : p * 64 + 64, :]
                even = even + pltpu.roll(even, 64, 1)
                odd = odd + pltpu.roll(odd, 64, 1)
                place = w * 512 + p * 128
                contrib[h, :, place : place + 128] = jnp.where(first, even, odd).astype(BF16)
        return carry

    lax.fori_loop(0, bricks // 2, gather, 0)


VMEM = pl.BlockSpec(memory_space=pltpu.VMEM)
SMEM = pl.BlockSpec(memory_space=pltpu.SMEM)


def per_device(
    bricks,
    positions,
    spacing,
    brick_ids,
    region_rank,
    target,
    in_weight,
    in_bias,
    out_weight,
    out_bias,
):
    samples, rays = spacing.shape
    tiles = rays // 128
    channels, own_voxels = bricks.shape
    helpers = lax.axis_size("helper")
    regions = lax.axis_size("region")
    brick_count = helpers * own_voxels // 512

    copies = jnp.broadcast_to(bricks[None], (helpers, channels, own_voxels))
    table = lax.all_to_all(copies, "helper", 0, 0)

    in_b = in_bias[:, None]
    out_w = jnp.concatenate([out_weight, jnp.zeros_like(out_weight)], axis=0)
    out_b = jnp.concatenate([out_bias, jnp.zeros_like(out_bias)])[:, None]
    out_w3 = jnp.concatenate([out_weight] * 3 + [jnp.zeros_like(out_weight)], axis=0).T
    rank = region_rank.T
    region = lax.axis_index("region").astype(jnp.int32)[None]

    segments, feature, decoded, places = pl.pallas_call(
        forward_kernel,
        out_shape=(
            jax.ShapeDtypeStruct((regions, 4 * tiles, 128), F32),
            jax.ShapeDtypeStruct((samples, channels, rays), BF16),
            jax.ShapeDtypeStruct((4, samples, rays), F32),
            jax.ShapeDtypeStruct((samples * tiles, 8, 128), F32),
        ),
        in_specs=[SMEM] + [VMEM] * 7,
        out_specs=(VMEM, VMEM, VMEM, VMEM),
        scratch_shapes=[
            pltpu.VMEM((brick_count, 256, 128), BF16),
            pltpu.VMEM((samples, 8, rays), F32),
            pltpu.VMEM((samples, rays), F32),
        ],
        name="forward",
    )(brick_ids, table, positions, spacing, in_weight, in_b, out_w, out_b)

    exchanged = lax.all_to_all(segments, "region", 0, 0)

    colour, contribution = pl.pallas_call(
        backward_kernel,
        out_shape=(
            jax.ShapeDtypeStruct((3, rays), F32),
            jax.ShapeDtypeStruct((helpers, channels, own_voxels), BF16),
        ),
        in_specs=[SMEM, SMEM] + [VMEM] * 10,
        out_specs=(VMEM, VMEM),
        scratch_shapes=[
            pltpu.VMEM((brick_count, 256, 128), F32),
            pltpu.VMEM((8, rays), F32),
            pltpu.VMEM((4, samples, rays), F32),
            pltpu.VMEM((samples, 4, rays), F32),
            pltpu.VMEM((samples, rays), F32),
        ],
        name="backward",
    )(
        brick_ids,
        region,
        exchanged.reshape(regions * 4 * tiles, 128),
        rank,
        target,
        decoded,
        feature,
        places,
        spacing,
        in_weight,
        in_b,
        out_w3,
    )
    received = lax.all_to_all(contribution, "helper", 0, 0)
    brick_grad = jnp.sum(received.astype(F32), axis=0)
    return colour, brick_grad


def solution(mesh):
    placed = (
        P(None, ("region", "helper")),
        P(None, "region", "helper"),
        P("region", "helper"),
        P("region", "helper"),
        P("helper", None),
        P(None, "helper"),
        P(),
        P(),
        P(),
        P(),
    )
    return jax.shard_map(
        per_device,
        mesh=mesh,
        in_specs=placed,
        out_specs=(P(None, "helper"), P(None, ("region", "helper"))),
        check_vma=False,
    )
```

```python
import jax
import jax.numpy as jnp
from jax import lax
from jax.experimental import pallas as pl
from jax.experimental.pallas import tpu as pltpu
from jax.sharding import PartitionSpec as P

F32 = jnp.float32
BF16 = jnp.bfloat16


def sigmoid(v):
    return 0.5 * jnp.tanh(0.5 * v) + 0.5


def diagonal(block, copies):
    rows, columns = block.shape
    wide = jnp.concatenate([block] * copies, axis=1)
    place = lax.broadcasted_iota(jnp.int32, (rows, columns * copies), 1) // columns
    return jnp.concatenate([jnp.where(place == k, wide, 0.0) for k in range(copies)], axis=0)


def weights_kernel(pos, half_w, out_w, out_w3, back_w, hats, planes, mats_far, mats, stored):
    samples, rays = pos.shape[1:]
    tiles = rays // 128
    mats[0:512, :] = diagonal(half_w[...].astype(F32), 8).astype(BF16)
    mats[512:544, :] = diagonal(out_w[...].astype(F32), 4).astype(BF16)
    mats[544:672, :] = diagonal(back_w[...].astype(F32), 4).astype(BF16)
    mats[672:1184, 0:128] = diagonal(out_w3[...].astype(F32), 8).astype(BF16)
    mats[672:1184, 128:256] = jnp.zeros((512, 128), BF16)
    store = pltpu.make_async_copy(mats, mats_far, stored)
    store.start()
    grid = lax.broadcasted_iota(jnp.int32, (8, 128), 0).astype(F32)
    for s in range(samples):
        for j in range(tiles):
            lanes = slice(j * 128, (j + 1) * 128)
            x, y, z = [pos[d, s : s + 1, lanes] for d in range(3)]
            hats[s * tiles + j] = jnp.maximum(1.0 - jnp.abs(x - grid), 0.0)
            wz = jnp.maximum(1.0 - jnp.abs(z - grid), 0.0)
            both = [jnp.maximum(1.0 - jnp.abs(y - float(g)), 0.0) * wz for g in range(8)]
            both = jnp.concatenate(both, axis=0)
            high = both.astype(BF16)
            planes[s * tiles + j, 0:64, :] = high
            planes[s * tiles + j, 64:128, :] = (both - high.astype(F32)).astype(BF16)
    store.wait()


def forward_kernel(
    ids,
    table,
    hats,
    planes,
    in_b,
    out_b,
    mats_far,
    spc_far,
    seg,
    dec,
    slopes_far,
    mats,
    spc,
    slopes,
    doubled,
    heads,
    scan,
    fetched,
    stored,
):
    samples, rays = spc.shape
    tiles = rays // 128
    fetch_mats = pltpu.make_async_copy(mats_far.at[0:544], mats, fetched.at[0])
    fetch_spc = pltpu.make_async_copy(spc_far, spc, fetched.at[1])
    fetch_mats.start()
    fetch_spc.start()

    def spread(h, carry):
        for w in range(2):
            for x in range(8):
                part = table[h, :, w * 512 + x * 64 : w * 512 + (x + 1) * 64]
                doubled[h * 2 + w, x * 32 : (x + 1) * 32, :] = jnp.concatenate([part, part], axis=1)
        return carry

    lax.fori_loop(0, table.shape[0], spread, 0, unroll=2)
    fetch_mats.wait()

    def group(g, carry):
        blocks = []
        for m in range(8):
            s = g * 4 + m // 2
            parts = []
            for n in range(2):
                j = m % 2 * 2 + n
                tile = s * tiles + j
                sums = jnp.dot(doubled[ids[s, j]], planes[tile], preferred_element_type=F32)
                part = hats[tile, 0:1, :] * sums[0:32, :]
                for x in range(1, 8):
                    part = part + hats[tile, x : x + 1, :] * sums[x * 32 : (x + 1) * 32, :]
                parts.append(part.astype(BF16))
            blocks.append(jnp.concatenate(parts, axis=1))
        halves = jnp.dot(mats[0:512, :], jnp.concatenate(blocks, axis=0), preferred_element_type=F32)
        hidden = []
        for m in range(8):
            half = halves[m * 64 : (m + 1) * 64, :] + in_b[...]
            bend = jnp.tanh(half)
            slopes[g, m * 64 : (m + 1) * 64, :] = (1.0 + bend) * (1.0 + half * (1.0 - bend))
            hidden.append((half + half * bend).astype(BF16))
        for q in range(2):
            quad = jnp.concatenate(hidden[q * 4 : q * 4 + 4], axis=0)
            decoded = jnp.dot(mats[512:544, :], quad, preferred_element_type=F32)
            for i in range(4):
                m = q * 4 + i
                lanes = slice(m % 2 * 256, m % 2 * 256 + 256)
                heads[g * 4 + m // 2, :, lanes] = decoded[i * 8 : i * 8 + 8, :] + out_b[...]
        pltpu.make_async_copy(slopes.at[g], slopes_far.at[g], stored.at[g]).start()
        return carry

    lax.fori_loop(0, samples // 4, group, 0, unroll=4)

    for s in range(samples):
        for c in range(4):
            dec[c, s : s + 1, :] = heads[s, c : c + 1, :]
    fetch_spc.wait()
    raw = dec[0]
    density = jnp.maximum(raw, 0.0) + jnp.log1p(jnp.exp(-jnp.abs(raw)))
    thickness = density * spc[...]
    total = jnp.zeros((1, rays), F32)
    for s in range(samples):
        scan[s : s + 1, :] = total
        total = total + thickness[s : s + 1, :]
    weight = jnp.exp(-scan[...]) * (1.0 - jnp.exp(-thickness))
    rows = [-total]
    for c in range(1, 4):
        rows.append(jnp.sum(weight * sigmoid(dec[c]), axis=0, keepdims=True))
    own = jnp.concatenate(
        [rows[c][:, j * 128 : (j + 1) * 128] for j in range(tiles) for c in range(4)], axis=0
    )
    seg[...] = jnp.broadcast_to(own[None], seg.shape)
    for g in range(samples // 4):
        pltpu.make_async_copy(slopes.at[g], slopes_far.at[g], stored.at[g]).wait()


def backward_kernel(
    ids,
    region,
    segs,
    rank,
    target,
    hats,
    planes,
    dec,
    slopes_far,
    mats_far,
    spc_far,
    colour,
    contrib,
    slopes,
    mats,
    spc,
    total,
    back,
    heads,
    scan,
    fetched,
):
    samples, rays = spc.shape
    fetch_spc = pltpu.make_async_copy(spc_far, spc, fetched.at[0])
    fetch_slopes = pltpu.make_async_copy(slopes_far, slopes, fetched.at[1])
    fetch_mats = pltpu.make_async_copy(mats_far.at[544:1184], mats, fetched.at[2])
    fetch_spc.start()
    fetch_mats.start()
    fetch_slopes.start()
    tiles = rays // 128
    regions = rank.shape[0]
    bricks = total.shape[0]
    stride = segs.shape[0] // regions

    for b in range(bricks):
        total[b] = jnp.zeros(total.shape[1:], F32)

    for j in range(tiles):
        lanes = slice(j * 128, (j + 1) * 128)
        logs = segs[pl.ds(j * 4, regions, stride), :]
        order = rank[:, lanes]
        before = jnp.zeros((regions, 128), F32)
        for i in range(regions):
            log_i = segs[i * stride + j * 4 : i * stride + j * 4 + 1, :]
            before = before + jnp.where(rank[i : i + 1, lanes] < order, log_i, 0.0)
        fading = jnp.exp(before)
        row = lax.broadcasted_iota(jnp.int32, (regions, 128), 0)
        order_own = jnp.sum(jnp.where(row == region[0], order, 0), axis=0, keepdims=True)
        fading_own = jnp.sum(jnp.where(row == region[0], fading, 0.0), axis=0, keepdims=True)
        log_grad = jnp.zeros((1, 128), F32)
        for c in range(3):
            part = fading * segs[pl.ds(j * 4 + c + 1, regions, stride), :]
            seen = jnp.sum(part, axis=0, keepdims=True)
            behind = jnp.sum(jnp.where(order > order_own, part, 0.0), axis=0, keepdims=True)
            colour[c : c + 1, lanes] = seen
            residual = seen - target[c : c + 1, lanes]
            log_grad = log_grad + residual * behind
            back[c + 1 : c + 2, lanes] = fading_own * residual
        back[0:1, lanes] = log_grad

    fetch_spc.wait()
    raw = dec[0]
    density = jnp.maximum(raw, 0.0) + jnp.log1p(jnp.exp(-jnp.abs(raw)))
    thickness = density * spc[...]
    run = jnp.zeros((1, rays), F32)
    for s in range(samples):
        scan[s : s + 1, :] = run
        run = run + thickness[s : s + 1, :]
    entering = jnp.exp(-scan[...])
    through = jnp.exp(-thickness)
    weight = entering * (1.0 - through)
    mixing = jnp.zeros((samples, rays), F32)
    grads = [None] * 4
    for c in range(3):
        grad_col = back[c + 1 : c + 2, :]
        radiance = sigmoid(dec[c + 1])
        mixing = mixing + grad_col * radiance
        grads[c + 1] = weight * radiance * (1.0 - radiance) * grad_col
    weighted = weight * mixing
    run = jnp.zeros((1, rays), F32)
    for s in reversed(range(samples)):
        scan[s : s + 1, :] = run
        run = run + weighted[s : s + 1, :]
    grads[0] = (entering * through * mixing - scan[...] - back[0:1, :]) * spc[...] * sigmoid(raw)
    for c in range(4):
        high = grads[c].astype(BF16).astype(F32)
        rest = grads[c] - high
        middle = rest.astype(BF16).astype(F32)
        low = rest - middle
        for k, piece in enumerate((high, middle, low)):
            for s in range(samples):
                for h in range(2):
                    row = (s % 4 * 2 + h) * 16 + k * 4 + c
                    heads[s // 4, row : row + 1, :] = piece[s : s + 1, h * 256 : h * 256 + 256]
    for g in range(samples // 4):
        for m in range(8):
            heads[g, m * 16 + 12 : m * 16 + 16, :] = jnp.zeros((4, 256), F32)

    fetch_mats.wait()
    fetch_slopes.wait()

    def group(g, carry):
        hidden = jnp.dot(mats[128:640, 0:128], heads[g].astype(BF16), preferred_element_type=F32)
        for q in range(2):
            rows = slice(q * 256, q * 256 + 256)
            grad_in = (hidden[rows, :] * slopes[g, rows, :]).astype(BF16)
            grad_feature = jnp.dot(mats[0:128, :], grad_in, preferred_element_type=F32)
            for i in range(4):
                for n in range(2):
                    m = q * 4 + i
                    s, j = g * 4 + m // 2, m % 2 * 2 + n
                    tile = s * tiles + j
                    own = grad_feature[i * 32 : i * 32 + 32, n * 128 : n * 128 + 128]
                    blocks = [(hats[tile, x : x + 1, :] * own).astype(BF16) for x in range(8)]
                    total[ids[s, j]] += lax.dot_general(
                        jnp.concatenate(blocks, axis=0),
                        planes[tile],
                        (((1,), (1,)), ((), ())),
                        preferred_element_type=F32,
                    )
        return carry

    lax.fori_loop(0, samples // 4, group, 0, unroll=4)

    first = lax.broadcasted_iota(jnp.int32, (32, 128), 1) < 64

    def gather(h, carry):
        for w in range(2):
            for p in range(4):
                even = total[h * 2 + w, p * 64 : p * 64 + 32, :]
                odd = total[h * 2 + w, p * 64 + 32 : p * 64 + 64, :]
                keep = jnp.where(first, even, odd)
                move = jnp.where(first, odd, even)
                place = w * 512 + p * 128
                contrib[h, :, place : place + 128] = (keep + pltpu.roll(move, 64, 1)).astype(BF16)
        return carry

    lax.fori_loop(0, bricks // 2, gather, 0, unroll=2)


VMEM = pl.BlockSpec(memory_space=pltpu.VMEM)
SMEM = pl.BlockSpec(memory_space=pltpu.SMEM)
HBM = pl.BlockSpec(memory_space=pltpu.HBM)


def shaped(*shape, dtype=F32):
    return jax.ShapeDtypeStruct(shape, dtype)


def far(*arrays):
    return [pltpu.with_memory_space_constraint(x, pltpu.HBM) for x in arrays]


def kernel(body, name, outs, smem, vmem, far, out_far, scratch, limit, flops):
    return pl.pallas_call(
        body,
        out_shape=outs,
        in_specs=[SMEM] * smem + [VMEM] * vmem + [HBM] * far,
        out_specs=(VMEM,) * (len(outs) - out_far) + (HBM,) * out_far,
        scratch_shapes=scratch,
        compiler_params=pltpu.CompilerParams(vmem_limit_bytes=limit << 20),
        cost_estimate=pl.CostEstimate(flops=flops, bytes_accessed=1 << 21, transcendentals=0),
        name=name,
    )


def per_device(
    bricks,
    positions,
    spacing,
    brick_ids,
    region_rank,
    target,
    in_weight,
    in_bias,
    out_weight,
    out_bias,
):
    samples, rays = spacing.shape
    tiles = rays // 128
    channels, own_voxels = bricks.shape
    hidden = in_weight.shape[0]
    helpers = lax.axis_size("helper")
    regions = lax.axis_size("region")
    brick_count = helpers * own_voxels // 512

    copies = jnp.broadcast_to(bricks[None], (helpers, channels, own_voxels))
    table = lax.all_to_all(copies, "helper", 0, 0)

    half_w = in_weight * 0.5
    half_b = (in_bias * 0.5)[:, None]
    out_w = jnp.concatenate([out_weight, jnp.zeros_like(out_weight)], axis=0)
    out_b = jnp.concatenate([out_bias, jnp.zeros_like(out_bias)])[:, None]
    half_out = out_weight * 0.5
    out_w3 = jnp.concatenate([half_out] * 3 + [jnp.zeros_like(half_out)], axis=0).T
    rank = region_rank.T
    region = lax.axis_index("region").astype(jnp.int32)[None]

    hats, planes, mats = kernel(
        weights_kernel,
        "weights",
        (
            shaped(samples * tiles, 8, 128),
            shaped(samples * tiles, 128, 128, dtype=BF16),
            pltpu.HBM((1184, 256), BF16),
        ),
        0,
        5,
        0,
        1,
        [pltpu.VMEM((1184, 256), BF16), pltpu.SemaphoreType.DMA],
        8,
        1 << 24,
    )(positions, half_w, out_w, out_w3, in_weight.T)

    segments, decoded, slopes = kernel(
        forward_kernel,
        "forward",
        (
            shaped(regions, 4 * tiles, 128),
            shaped(4, samples, rays),
            pltpu.HBM((samples // 4, 8 * hidden, 256), F32),
        ),
        1,
        5,
        2,
        1,
        [
            pltpu.VMEM((544, 256), BF16),
            pltpu.VMEM((samples, rays), F32),
            pltpu.VMEM((samples // 4, 8 * hidden, 256), F32),
            pltpu.VMEM((brick_count, 256, 128), BF16),
            pltpu.VMEM((samples, 8, rays), F32),
            pltpu.VMEM((samples, rays), F32),
            pltpu.SemaphoreType.DMA((2,)),
            pltpu.SemaphoreType.DMA((samples // 4,)),
        ],
        12,
        1 << 28,
    )(brick_ids, table, hats, planes, half_b, out_b, *far(mats, spacing))

    exchanged = lax.all_to_all(segments, "region", 0, 0)

    colour, contribution = kernel(
        backward_kernel,
        "backward",
        (shaped(3, rays), shaped(helpers, channels, own_voxels, dtype=BF16)),
        2,
        6,
        3,
        0,
        [
            pltpu.VMEM((samples // 4, 8 * hidden, 256), F32),
            pltpu.VMEM((640, 256), BF16),
            pltpu.VMEM((samples, rays), F32),
            pltpu.VMEM((brick_count, 256, 128), F32),
            pltpu.VMEM((8, rays), F32),
            pltpu.VMEM((samples // 4, 128, 256), F32),
            pltpu.VMEM((samples, rays), F32),
            pltpu.SemaphoreType.DMA((3,)),
        ],
        16,
        1 << 28,
    )(
        brick_ids,
        region,
        exchanged.reshape(regions * 4 * tiles, 128),
        rank,
        target,
        hats,
        planes,
        decoded,
        *far(slopes, mats, spacing),
    )
    received = lax.all_to_all(contribution, "helper", 0, 0)
    brick_grad = jnp.sum(received.astype(F32), axis=0)
    return colour, brick_grad


def solution(mesh):
    placed = (
        P(None, ("region", "helper")),
        P(None, "region", "helper"),
        P("region", "helper"),
        P("region", "helper"),
        P("helper", None),
        P(None, "helper"),
        P(),
        P(),
        P(),
        P(),
    )
    return jax.shard_map(
        per_device,
        mesh=mesh,
        in_specs=placed,
        out_specs=(P(None, "helper"), P(None, ("region", "helper"))),
        check_vma=False,
    )
```

```python
import jax
import jax.numpy as jnp
from jax import lax
from jax.experimental import pallas as pl
from jax.experimental.pallas import tpu as pltpu
from jax.sharding import PartitionSpec as P

F32 = jnp.float32
BF16 = jnp.bfloat16


def sigmoid(v):
    return 0.5 * jnp.tanh(0.5 * v) + 0.5


def diagonal(block, copies):
    rows, columns = block.shape
    wide = jnp.concatenate([block] * copies, axis=1)
    place = lax.broadcasted_iota(jnp.int32, (rows, columns * copies), 1) // columns
    return jnp.concatenate([jnp.where(place == k, wide, 0.0) for k in range(copies)], axis=0)


def weights_kernel(pos, half_w, out_w, out_w3, back_w, hats, planes, mats_far, mats, stored):
    samples, rays = pos.shape[1:]
    tiles = rays // 128
    mats[0:512, :] = diagonal(half_w[...].astype(F32), 8).astype(BF16)
    mats[512:544, :] = diagonal(out_w[...].astype(F32), 4).astype(BF16)
    mats[544:672, :] = diagonal(back_w[...].astype(F32), 4).astype(BF16)
    mats[672:1184, 0:128] = diagonal(out_w3[...].astype(F32), 8).astype(BF16)
    mats[672:1184, 128:256] = jnp.zeros((512, 128), BF16)
    store = pltpu.make_async_copy(mats, mats_far, stored)
    store.start()
    grid = lax.broadcasted_iota(jnp.int32, (8, 128), 0).astype(F32)
    for s in range(samples):
        for j in range(tiles):
            lanes = slice(j * 128, (j + 1) * 128)
            x, y, z = [pos[d, s : s + 1, lanes] for d in range(3)]
            hats[s * tiles + j] = jnp.maximum(1.0 - jnp.abs(x - grid), 0.0)
            wz = jnp.maximum(1.0 - jnp.abs(z - grid), 0.0)
            both = [jnp.maximum(1.0 - jnp.abs(y - float(g)), 0.0) * wz for g in range(8)]
            both = jnp.concatenate(both, axis=0)
            high = both.astype(BF16)
            planes[s * tiles + j, 0:64, :] = high
            planes[s * tiles + j, 64:128, :] = (both - high.astype(F32)).astype(BF16)
    store.wait()


def forward_kernel(
    region,
    table,
    hats,
    planes,
    in_b,
    out_b,
    mats_far,
    spc_far,
    ids_far,
    seg,
    dec,
    slopes,
    mats,
    spc,
    ids,
    doubled,
    heads,
    scan,
    fetched,
):
    samples, rays = spc.shape
    tiles = rays // 128
    fetch_mats = pltpu.make_async_copy(mats_far.at[0:544], mats, fetched.at[0])
    fetch_spc = pltpu.make_async_copy(spc_far, spc, fetched.at[1])
    fetch_ids = pltpu.make_async_copy(ids_far, ids, fetched.at[2])
    fetch_ids.start()
    fetch_mats.start()
    fetch_spc.start()

    def spread(h, carry):
        for w in range(2):
            for x in range(8):
                part = table[h, :, w * 512 + x * 64 : w * 512 + (x + 1) * 64]
                doubled[h * 2 + w, x * 32 : (x + 1) * 32, :] = jnp.concatenate([part, part], axis=1)
        return carry

    lax.fori_loop(0, table.shape[0], spread, 0, unroll=4)
    fetch_ids.wait()
    fetch_mats.wait()

    def group(g, carry):
        blocks = []
        for m in range(8):
            s = g * 4 + m // 2
            parts = []
            for n in range(2):
                j = m % 2 * 2 + n
                tile = s * tiles + j
                sums = jnp.dot(doubled[ids[s, j]], planes[tile], preferred_element_type=F32)
                part = hats[tile, 0:1, :] * sums[0:32, :]
                for x in range(1, 8):
                    part = part + hats[tile, x : x + 1, :] * sums[x * 32 : (x + 1) * 32, :]
                parts.append(part.astype(BF16))
            blocks.append(jnp.concatenate(parts, axis=1))
        halves = jnp.dot(mats[0:512, :], jnp.concatenate(blocks, axis=0), preferred_element_type=F32)
        hidden = []
        for m in range(8):
            half = halves[m * 64 : (m + 1) * 64, :] + in_b[...]
            bend = jnp.tanh(half)
            slopes[g, m * 64 : (m + 1) * 64, :] = (1.0 + bend) * (1.0 + half * (1.0 - bend))
            hidden.append((half + half * bend).astype(BF16))
        for q in range(2):
            quad = jnp.concatenate(hidden[q * 4 : q * 4 + 4], axis=0)
            decoded = jnp.dot(mats[512:544, :], quad, preferred_element_type=F32)
            for i in range(4):
                m = q * 4 + i
                lanes = slice(m % 2 * 256, m % 2 * 256 + 256)
                heads[g * 4 + m // 2, :, lanes] = decoded[i * 8 : i * 8 + 8, :] + out_b[...]
        return carry

    lax.fori_loop(0, samples // 4, group, 0, unroll=4)

    for s in range(samples):
        for c in range(4):
            dec[c, s : s + 1, :] = heads[s, c : c + 1, :]
    fetch_spc.wait()
    raw = dec[0]
    density = jnp.maximum(raw, 0.0) + jnp.log1p(jnp.exp(-jnp.abs(raw)))
    thickness = density * spc[...]
    total = jnp.zeros((1, rays), F32)
    for s in range(samples):
        scan[s : s + 1, :] = total
        total = total + thickness[s : s + 1, :]
    weight = jnp.exp(-scan[...]) * (1.0 - jnp.exp(-thickness))
    rows = [-total]
    for c in range(1, 4):
        rows.append(jnp.sum(weight * sigmoid(dec[c]), axis=0, keepdims=True))
    own = jnp.concatenate(
        [rows[c][:, j * 128 : (j + 1) * 128] for j in range(tiles) for c in range(4)], axis=0
    )
    seg[...] = jnp.broadcast_to(own[None], seg.shape)


def backward_kernel(
    region,
    segs,
    rank,
    target,
    hats,
    planes,
    dec,
    slopes,
    mats_far,
    spc_far,
    ids_far,
    contrib,
    colour_far,
    mats,
    spc,
    ids,
    colour,
    total,
    back,
    heads,
    scan,
    fetched,
):
    samples, rays = spc.shape
    fetch_spc = pltpu.make_async_copy(spc_far, spc, fetched.at[0])
    fetch_mats = pltpu.make_async_copy(mats_far.at[544:1184], mats, fetched.at[1])
    fetch_ids = pltpu.make_async_copy(ids_far, ids, fetched.at[2])
    store_colour = pltpu.make_async_copy(colour, colour_far, fetched.at[3])
    fetch_spc.start()
    fetch_ids.start()
    fetch_mats.start()
    tiles = rays // 128
    regions = rank.shape[0]
    bricks = total.shape[0]
    stride = segs.shape[0] // regions

    for b in range(bricks):
        total[b] = jnp.zeros(total.shape[1:], F32)

    for j in range(tiles):
        lanes = slice(j * 128, (j + 1) * 128)
        logs = segs[pl.ds(j * 4, regions, stride), :]
        order = rank[:, lanes]
        before = jnp.zeros((regions, 128), F32)
        for i in range(regions):
            log_i = segs[i * stride + j * 4 : i * stride + j * 4 + 1, :]
            before = before + jnp.where(rank[i : i + 1, lanes] < order, log_i, 0.0)
        fading = jnp.exp(before)
        row = lax.broadcasted_iota(jnp.int32, (regions, 128), 0)
        order_own = jnp.sum(jnp.where(row == region[0], order, 0), axis=0, keepdims=True)
        fading_own = jnp.sum(jnp.where(row == region[0], fading, 0.0), axis=0, keepdims=True)
        log_grad = jnp.zeros((1, 128), F32)
        for c in range(3):
            part = fading * segs[pl.ds(j * 4 + c + 1, regions, stride), :]
            seen = jnp.sum(part, axis=0, keepdims=True)
            behind = jnp.sum(jnp.where(order > order_own, part, 0.0), axis=0, keepdims=True)
            colour[c : c + 1, lanes] = seen
            residual = seen - target[c : c + 1, lanes]
            log_grad = log_grad + residual * behind
            back[c + 1 : c + 2, lanes] = fading_own * residual
        back[0:1, lanes] = log_grad

    store_colour.start()
    fetch_spc.wait()
    raw = dec[0]
    density = jnp.maximum(raw, 0.0) + jnp.log1p(jnp.exp(-jnp.abs(raw)))
    thickness = density * spc[...]
    run = jnp.zeros((1, rays), F32)
    for s in range(samples):
        scan[s : s + 1, :] = run
        run = run + thickness[s : s + 1, :]
    entering = jnp.exp(-scan[...])
    through = jnp.exp(-thickness)
    weight = entering * (1.0 - through)
    mixing = jnp.zeros((samples, rays), F32)
    grads = [None] * 4
    for c in range(3):
        grad_col = back[c + 1 : c + 2, :]
        radiance = sigmoid(dec[c + 1])
        mixing = mixing + grad_col * radiance
        grads[c + 1] = weight * radiance * (1.0 - radiance) * grad_col
    weighted = weight * mixing
    run = jnp.zeros((1, rays), F32)
    for s in reversed(range(samples)):
        scan[s : s + 1, :] = run
        run = run + weighted[s : s + 1, :]
    grads[0] = (entering * through * mixing - scan[...] - back[0:1, :]) * spc[...] * sigmoid(raw)
    for c in range(4):
        high = grads[c].astype(BF16).astype(F32)
        rest = grads[c] - high
        middle = rest.astype(BF16).astype(F32)
        low = rest - middle
        for k, piece in enumerate((high, middle, low)):
            for s in range(samples):
                for h in range(2):
                    row = (s % 4 * 2 + h) * 16 + k * 4 + c
                    heads[s // 4, row : row + 1, :] = piece[s : s + 1, h * 256 : h * 256 + 256]
    for g in range(samples // 4):
        for m in range(8):
            heads[g, m * 16 + 12 : m * 16 + 16, :] = jnp.zeros((4, 256), F32)

    fetch_ids.wait()
    fetch_mats.wait()

    def group(g, carry):
        hidden = jnp.dot(mats[128:640, 0:128], heads[g].astype(BF16), preferred_element_type=F32)
        for q in range(2):
            rows = slice(q * 256, q * 256 + 256)
            grad_in = (hidden[rows, :] * slopes[g, rows, :]).astype(BF16)
            grad_feature = jnp.dot(mats[0:128, :], grad_in, preferred_element_type=F32)
            for i in range(4):
                for n in range(2):
                    m = q * 4 + i
                    s, j = g * 4 + m // 2, m % 2 * 2 + n
                    tile = s * tiles + j
                    own = grad_feature[i * 32 : i * 32 + 32, n * 128 : n * 128 + 128]
                    high, low = [], []
                    for x in range(8):
                        block = hats[tile, x : x + 1, :] * own
                        high.append(block.astype(BF16))
                        low.append((block - high[x].astype(F32)).astype(BF16))
                    both = [jnp.concatenate(high, axis=0), jnp.concatenate(low, axis=0)]
                    total[ids[s, j]] += lax.dot_general(
                        jnp.concatenate(both, axis=1),
                        jnp.concatenate([planes[tile]] * 2, axis=1),
                        (((1,), (1,)), ((), ())),
                        preferred_element_type=F32,
                    )
        return carry

    lax.fori_loop(0, samples // 4, group, 0, unroll=4)

    first = lax.broadcasted_iota(jnp.int32, (32, 128), 1) < 64

    def gather(h, carry):
        for w in range(2):
            for p in range(4):
                even = total[h * 2 + w, p * 64 : p * 64 + 32, :]
                odd = total[h * 2 + w, p * 64 + 32 : p * 64 + 64, :]
                keep = jnp.where(first, even, odd)
                move = jnp.where(first, odd, even)
                place = w * 512 + p * 128
                contrib[h, :, place : place + 128] = (keep + pltpu.roll(move, 64, 1)).astype(BF16)
        return carry

    lax.fori_loop(0, bricks // 2, gather, 0, unroll=8)
    store_colour.wait()


VMEM = pl.BlockSpec(memory_space=pltpu.VMEM)
SMEM = pl.BlockSpec(memory_space=pltpu.SMEM)
HBM = pl.BlockSpec(memory_space=pltpu.HBM)


def shaped(*shape, dtype=F32):
    return jax.ShapeDtypeStruct(shape, dtype)


def far(*arrays):
    return [pltpu.with_memory_space_constraint(x, pltpu.HBM) for x in arrays]


def kernel(body, name, outs, smem, vmem, far, out_far, scratch, limit, flops):
    return pl.pallas_call(
        body,
        out_shape=outs,
        in_specs=[SMEM] * smem + [VMEM] * vmem + [HBM] * far,
        out_specs=(VMEM,) * (len(outs) - out_far) + (HBM,) * out_far,
        scratch_shapes=scratch,
        compiler_params=pltpu.CompilerParams(vmem_limit_bytes=limit << 20),
        cost_estimate=pl.CostEstimate(flops=flops, bytes_accessed=1 << 21, transcendentals=0),
        name=name,
    )


def per_device(
    bricks,
    positions,
    spacing,
    brick_ids,
    region_rank,
    target,
    in_weight,
    in_bias,
    out_weight,
    out_bias,
):
    samples, rays = spacing.shape
    tiles = rays // 128
    channels, own_voxels = bricks.shape
    hidden = in_weight.shape[0]
    helpers = lax.axis_size("helper")
    regions = lax.axis_size("region")
    brick_count = helpers * own_voxels // 512

    copies = jnp.broadcast_to(bricks[None], (helpers, channels, own_voxels))
    table = lax.all_to_all(copies, "helper", 0, 0)

    half_w = in_weight * 0.5
    half_b = (in_bias * 0.5)[:, None]
    out_w = jnp.concatenate([out_weight, jnp.zeros_like(out_weight)], axis=0)
    out_b = jnp.concatenate([out_bias, jnp.zeros_like(out_bias)])[:, None]
    half_out = out_weight * 0.5
    out_w3 = jnp.concatenate([half_out] * 3 + [jnp.zeros_like(half_out)], axis=0).T
    rank = region_rank.T
    region = lax.axis_index("region").astype(jnp.int32)[None]

    hats, planes, mats = kernel(
        weights_kernel,
        "weights",
        (
            shaped(samples * tiles, 8, 128),
            shaped(samples * tiles, 128, 128, dtype=BF16),
            pltpu.HBM((1184, 256), BF16),
        ),
        0,
        5,
        0,
        1,
        [pltpu.VMEM((1184, 256), BF16), pltpu.SemaphoreType.DMA],
        8,
        1 << 24,
    )(positions, half_w, out_w, out_w3, in_weight.T)

    segments, decoded, slopes = kernel(
        forward_kernel,
        "forward",
        (
            shaped(regions, 4 * tiles, 128),
            shaped(4, samples, rays),
            shaped(samples // 4, 8 * hidden, 256),
        ),
        1,
        5,
        3,
        0,
        [
            pltpu.VMEM((544, 256), BF16),
            pltpu.VMEM((samples, rays), F32),
            pltpu.SMEM((samples, tiles), jnp.int32),
            pltpu.VMEM((brick_count, 256, 128), BF16),
            pltpu.VMEM((samples, 8, rays), F32),
            pltpu.VMEM((samples, rays), F32),
            pltpu.SemaphoreType.DMA((3,)),
        ],
        12,
        1 << 28,
    )(region, table, hats, planes, half_b, out_b, *far(mats, spacing, brick_ids))

    exchanged = lax.all_to_all(segments, "region", 0, 0)

    contribution, colour = kernel(
        backward_kernel,
        "backward",
        (shaped(helpers, channels, own_voxels, dtype=BF16), pltpu.HBM((3, rays), F32)),
        1,
        7,
        3,
        1,
        [
            pltpu.VMEM((640, 256), BF16),
            pltpu.VMEM((samples, rays), F32),
            pltpu.SMEM((samples, tiles), jnp.int32),
            pltpu.VMEM((3, rays), F32),
            pltpu.VMEM((brick_count, 256, 128), F32),
            pltpu.VMEM((8, rays), F32),
            pltpu.VMEM((samples // 4, 128, 256), F32),
            pltpu.VMEM((samples, rays), F32),
            pltpu.SemaphoreType.DMA((4,)),
        ],
        16,
        1 << 28,
    )(
        region,
        exchanged.reshape(regions * 4 * tiles, 128),
        rank,
        target,
        hats,
        planes,
        decoded,
        slopes,
        *far(mats, spacing, brick_ids),
    )
    received = lax.all_to_all(contribution, "helper", 0, 0)
    brick_grad = jnp.sum(received.astype(F32), axis=0)
    return colour, brick_grad


def solution(mesh):
    placed = (
        P(None, ("region", "helper")),
        P(None, "region", "helper"),
        P("region", "helper"),
        P("region", "helper"),
        P("helper", None),
        P(None, "helper"),
        P(),
        P(),
        P(),
        P(),
    )
    return jax.shard_map(
        per_device,
        mesh=mesh,
        in_specs=placed,
        out_specs=(P(None, "helper"), P(None, ("region", "helper"))),
        check_vma=False,
    )
```

```python
import jax
import jax.numpy as jnp
from jax import lax
from jax.experimental import pallas as pl
from jax.experimental.pallas import tpu as pltpu
from jax.sharding import PartitionSpec as P

F32 = jnp.float32
BF16 = jnp.bfloat16


def sigmoid(v):
    return 0.5 * jnp.tanh(0.5 * v) + 0.5


def diagonal(block, copies):
    rows, columns = block.shape
    wide = jnp.concatenate([block] * copies, axis=1)
    place = lax.broadcasted_iota(jnp.int32, (rows, columns * copies), 1) // columns
    return jnp.concatenate([jnp.where(place == k, wide, 0.0) for k in range(copies)], axis=0)


def weights_kernel(pos, half_w, out_w, out_w3, back_w, hats, planes, mats_far, mats, stored):
    samples, rays = pos.shape[1:]
    tiles = rays // 128
    mats[0:512, :] = diagonal(half_w[...].astype(F32), 8).astype(BF16)
    mats[512:544, :] = diagonal(out_w[...].astype(F32), 4).astype(BF16)
    mats[544:672, :] = diagonal(back_w[...].astype(F32), 4).astype(BF16)
    mats[672:1184, 0:128] = diagonal(out_w3[...].astype(F32), 8).astype(BF16)
    mats[672:1184, 128:256] = jnp.zeros((512, 128), BF16)
    store = pltpu.make_async_copy(mats, mats_far, stored)
    store.start()
    grid = lax.broadcasted_iota(jnp.int32, (8, 128), 0).astype(F32)
    for s in range(samples):
        for j in range(tiles):
            lanes = slice(j * 128, (j + 1) * 128)
            x, y, z = [pos[d, s : s + 1, lanes] for d in range(3)]
            hats[s * tiles + j] = jnp.maximum(1.0 - jnp.abs(x - grid), 0.0)
            wz = jnp.maximum(1.0 - jnp.abs(z - grid), 0.0)
            both = [jnp.maximum(1.0 - jnp.abs(y - float(g)), 0.0) * wz for g in range(8)]
            both = jnp.concatenate(both, axis=0)
            high = both.astype(BF16)
            planes[s * tiles + j, 0:64, :] = high
            planes[s * tiles + j, 64:128, :] = (both - high.astype(F32)).astype(BF16)
    store.wait()


def forward_kernel(
    region,
    table,
    hats,
    planes,
    in_b,
    out_b,
    mats_far,
    spc_far,
    ids_far,
    seg,
    dec,
    slopes,
    mats,
    spc,
    ids,
    doubled,
    heads,
    scan,
    fetched,
):
    samples, rays = spc.shape
    tiles = rays // 128
    fetch_mats = pltpu.make_async_copy(mats_far.at[0:544], mats, fetched.at[0])
    fetch_spc = pltpu.make_async_copy(spc_far, spc, fetched.at[1])
    fetch_ids = pltpu.make_async_copy(ids_far, ids, fetched.at[2])
    fetch_ids.start()
    fetch_mats.start()
    fetch_spc.start()

    def spread(h, carry):
        for w in range(2):
            for x in range(8):
                part = table[h, :, w * 512 + x * 64 : w * 512 + (x + 1) * 64]
                doubled[h * 2 + w, x * 32 : (x + 1) * 32, :] = jnp.concatenate([part, part], axis=1)
        return carry

    lax.fori_loop(0, table.shape[0], spread, 0, unroll=4)
    fetch_ids.wait()

    def group(g):
        blocks = []
        for m in range(8):
            s = g * 4 + m // 2
            parts = []
            for n in range(2):
                j = m % 2 * 2 + n
                tile = s * tiles + j
                sums = jnp.dot(doubled[ids[s, j]], planes[tile], preferred_element_type=F32)
                part = hats[tile, 0:1, :] * sums[0:32, :]
                for x in range(1, 8):
                    part = part + hats[tile, x : x + 1, :] * sums[x * 32 : (x + 1) * 32, :]
                parts.append(part.astype(BF16))
            blocks.append(jnp.concatenate(parts, axis=1))
        if g == 0:
            fetch_mats.wait()
        halves = jnp.dot(mats[0:512, :], jnp.concatenate(blocks, axis=0), preferred_element_type=F32)
        hidden = []
        for m in range(8):
            half = halves[m * 64 : (m + 1) * 64, :] + in_b[...]
            bend = jnp.tanh(half)
            slopes[g, m * 64 : (m + 1) * 64, :] = (1.0 + bend) * (1.0 + half * (1.0 - bend))
            hidden.append((half + half * bend).astype(BF16))
        for q in range(2):
            quad = jnp.concatenate(hidden[q * 4 : q * 4 + 4], axis=0)
            decoded = jnp.dot(mats[512:544, :], quad, preferred_element_type=F32)
            for i in range(4):
                m = q * 4 + i
                lanes = slice(m % 2 * 256, m % 2 * 256 + 256)
                heads[g * 4 + m // 2, :, lanes] = decoded[i * 8 : i * 8 + 8, :] + out_b[...]

    for g in range(samples // 4):
        group(g)

    for s in range(samples):
        for c in range(4):
            dec[c, s : s + 1, :] = heads[s, c : c + 1, :]
    fetch_spc.wait()
    raw = dec[0]
    density = jnp.maximum(raw, 0.0) + jnp.log1p(jnp.exp(-jnp.abs(raw)))
    thickness = density * spc[...]
    total = jnp.zeros((1, rays), F32)
    for s in range(samples):
        scan[s : s + 1, :] = total
        total = total + thickness[s : s + 1, :]
    weight = jnp.exp(-scan[...]) * (1.0 - jnp.exp(-thickness))
    rows = [-total]
    for c in range(1, 4):
        rows.append(jnp.sum(weight * sigmoid(dec[c]), axis=0, keepdims=True))
    own = jnp.concatenate(
        [rows[c][:, j * 128 : (j + 1) * 128] for j in range(tiles) for c in range(4)], axis=0
    )
    seg[...] = jnp.broadcast_to(own[None], seg.shape)


def backward_kernel(
    region,
    segs,
    rank,
    target,
    hats,
    planes,
    dec,
    slopes,
    mats_far,
    spc_far,
    ids_far,
    contrib,
    colour_far,
    mats,
    spc,
    ids,
    colour,
    total,
    back,
    heads,
    scan,
    fetched,
):
    samples, rays = spc.shape
    fetch_spc = pltpu.make_async_copy(spc_far, spc, fetched.at[0])
    fetch_mats = pltpu.make_async_copy(mats_far.at[544:1184], mats, fetched.at[1])
    fetch_ids = pltpu.make_async_copy(ids_far, ids, fetched.at[2])
    store_colour = pltpu.make_async_copy(colour, colour_far, fetched.at[3])
    fetch_spc.start()
    fetch_ids.start()
    fetch_mats.start()
    tiles = rays // 128
    regions = rank.shape[0]
    bricks = total.shape[0]
    stride = segs.shape[0] // regions

    for b in range(bricks):
        total[b] = jnp.zeros(total.shape[1:], F32)

    for j in range(tiles):
        lanes = slice(j * 128, (j + 1) * 128)
        logs = segs[pl.ds(j * 4, regions, stride), :]
        order = rank[:, lanes]
        before = jnp.zeros((regions, 128), F32)
        for i in range(regions):
            log_i = segs[i * stride + j * 4 : i * stride + j * 4 + 1, :]
            before = before + jnp.where(rank[i : i + 1, lanes] < order, log_i, 0.0)
        fading = jnp.exp(before)
        row = lax.broadcasted_iota(jnp.int32, (regions, 128), 0)
        order_own = jnp.sum(jnp.where(row == region[0], order, 0), axis=0, keepdims=True)
        fading_own = jnp.sum(jnp.where(row == region[0], fading, 0.0), axis=0, keepdims=True)
        log_grad = jnp.zeros((1, 128), F32)
        for c in range(3):
            part = fading * segs[pl.ds(j * 4 + c + 1, regions, stride), :]
            seen = jnp.sum(part, axis=0, keepdims=True)
            behind = jnp.sum(jnp.where(order > order_own, part, 0.0), axis=0, keepdims=True)
            colour[c : c + 1, lanes] = seen
            residual = seen - target[c : c + 1, lanes]
            log_grad = log_grad + residual * behind
            back[c + 1 : c + 2, lanes] = fading_own * residual
        back[0:1, lanes] = log_grad

    store_colour.start()
    fetch_spc.wait()
    raw = dec[0]
    density = jnp.maximum(raw, 0.0) + jnp.log1p(jnp.exp(-jnp.abs(raw)))
    thickness = density * spc[...]
    run = jnp.zeros((1, rays), F32)
    for s in range(samples):
        scan[s : s + 1, :] = run
        run = run + thickness[s : s + 1, :]
    entering = jnp.exp(-scan[...])
    through = jnp.exp(-thickness)
    weight = entering * (1.0 - through)
    mixing = jnp.zeros((samples, rays), F32)
    grads = [None] * 4
    for c in range(3):
        grad_col = back[c + 1 : c + 2, :]
        radiance = sigmoid(dec[c + 1])
        mixing = mixing + grad_col * radiance
        grads[c + 1] = weight * radiance * (1.0 - radiance) * grad_col
    weighted = weight * mixing
    run = jnp.zeros((1, rays), F32)
    for s in reversed(range(samples)):
        scan[s : s + 1, :] = run
        run = run + weighted[s : s + 1, :]
    grads[0] = (entering * through * mixing - scan[...] - back[0:1, :]) * spc[...] * sigmoid(raw)
    for c in range(4):
        high = grads[c].astype(BF16).astype(F32)
        rest = grads[c] - high
        middle = rest.astype(BF16).astype(F32)
        low = rest - middle
        for k, piece in enumerate((high, middle, low)):
            for s in range(samples):
                for h in range(2):
                    row = (s % 4 * 2 + h) * 16 + k * 4 + c
                    heads[s // 4, row : row + 1, :] = piece[s : s + 1, h * 256 : h * 256 + 256]
    for g in range(samples // 4):
        for m in range(8):
            heads[g, m * 16 + 12 : m * 16 + 16, :] = jnp.zeros((4, 256), F32)

    fetch_ids.wait()
    fetch_mats.wait()

    def group(g, carry):
        hidden = jnp.dot(mats[128:640, 0:128], heads[g].astype(BF16), preferred_element_type=F32)
        for q in range(2):
            rows = slice(q * 256, q * 256 + 256)
            grad_in = (hidden[rows, :] * slopes[g, rows, :]).astype(BF16)
            grad_feature = jnp.dot(mats[0:128, :], grad_in, preferred_element_type=F32)
            for i in range(4):
                for n in range(2):
                    m = q * 4 + i
                    s, j = g * 4 + m // 2, m % 2 * 2 + n
                    tile = s * tiles + j
                    own = grad_feature[i * 32 : i * 32 + 32, n * 128 : n * 128 + 128]
                    high, low = [], []
                    for x in range(8):
                        block = hats[tile, x : x + 1, :] * own
                        high.append(block.astype(BF16))
                        low.append((block - high[x].astype(F32)).astype(BF16))
                    both = [jnp.concatenate(high, axis=0), jnp.concatenate(low, axis=0)]
                    total[ids[s, j]] += lax.dot_general(
                        jnp.concatenate(both, axis=1),
                        jnp.concatenate([planes[tile]] * 2, axis=1),
                        (((1,), (1,)), ((), ())),
                        preferred_element_type=F32,
                    )
        return carry

    lax.fori_loop(0, samples // 4, group, 0, unroll=4)

    first = lax.broadcasted_iota(jnp.int32, (32, 128), 1) < 64

    def gather(h, carry):
        for w in range(2):
            for p in range(4):
                even = total[h * 2 + w, p * 64 : p * 64 + 32, :]
                odd = total[h * 2 + w, p * 64 + 32 : p * 64 + 64, :]
                keep = jnp.where(first, even, odd)
                move = jnp.where(first, odd, even)
                place = w * 512 + p * 128
                contrib[h, :, place : place + 128] = (keep + pltpu.roll(move, 64, 1)).astype(BF16)
        return carry

    lax.fori_loop(0, bricks // 2, gather, 0, unroll=8)
    store_colour.wait()


VMEM = pl.BlockSpec(memory_space=pltpu.VMEM)
SMEM = pl.BlockSpec(memory_space=pltpu.SMEM)
HBM = pl.BlockSpec(memory_space=pltpu.HBM)


def shaped(*shape, dtype=F32):
    return jax.ShapeDtypeStruct(shape, dtype)


def far(*arrays):
    return [pltpu.with_memory_space_constraint(x, pltpu.HBM) for x in arrays]


def kernel(body, name, outs, smem, vmem, far, out_far, scratch, limit, flops):
    return pl.pallas_call(
        body,
        out_shape=outs,
        in_specs=[SMEM] * smem + [VMEM] * vmem + [HBM] * far,
        out_specs=(VMEM,) * (len(outs) - out_far) + (HBM,) * out_far,
        scratch_shapes=scratch,
        compiler_params=pltpu.CompilerParams(vmem_limit_bytes=limit << 20),
        cost_estimate=pl.CostEstimate(flops=flops, bytes_accessed=1 << 21, transcendentals=0),
        name=name,
    )


def per_device(
    bricks,
    positions,
    spacing,
    brick_ids,
    region_rank,
    target,
    in_weight,
    in_bias,
    out_weight,
    out_bias,
):
    samples, rays = spacing.shape
    tiles = rays // 128
    channels, own_voxels = bricks.shape
    hidden = in_weight.shape[0]
    helpers = lax.axis_size("helper")
    regions = lax.axis_size("region")
    brick_count = helpers * own_voxels // 512

    copies = jnp.broadcast_to(bricks[None], (helpers, channels, own_voxels))
    table = lax.all_to_all(copies, "helper", 0, 0)

    half_w = in_weight * 0.5
    half_b = (in_bias * 0.5)[:, None]
    out_w = jnp.concatenate([out_weight, jnp.zeros_like(out_weight)], axis=0)
    out_b = jnp.concatenate([out_bias, jnp.zeros_like(out_bias)])[:, None]
    half_out = out_weight * 0.5
    out_w3 = jnp.concatenate([half_out] * 3 + [jnp.zeros_like(half_out)], axis=0).T
    rank = region_rank.T
    region = lax.axis_index("region").astype(jnp.int32)[None]

    hats, planes, mats = kernel(
        weights_kernel,
        "weights",
        (
            shaped(samples * tiles, 8, 128),
            shaped(samples * tiles, 128, 128, dtype=BF16),
            pltpu.HBM((1184, 256), BF16),
        ),
        0,
        5,
        0,
        1,
        [pltpu.VMEM((1184, 256), BF16), pltpu.SemaphoreType.DMA],
        8,
        1 << 24,
    )(positions, half_w, out_w, out_w3, in_weight.T)

    segments, decoded, slopes = kernel(
        forward_kernel,
        "forward",
        (
            shaped(regions, 4 * tiles, 128),
            shaped(4, samples, rays),
            shaped(samples // 4, 8 * hidden, 256),
        ),
        1,
        5,
        3,
        0,
        [
            pltpu.VMEM((544, 256), BF16),
            pltpu.VMEM((samples, rays), F32),
            pltpu.SMEM((samples, tiles), jnp.int32),
            pltpu.VMEM((brick_count, 256, 128), BF16),
            pltpu.VMEM((samples, 8, rays), F32),
            pltpu.VMEM((samples, rays), F32),
            pltpu.SemaphoreType.DMA((3,)),
        ],
        12,
        1 << 28,
    )(region, table, hats, planes, half_b, out_b, *far(mats, spacing, brick_ids))

    exchanged = lax.all_to_all(segments, "region", 0, 0)

    contribution, colour = kernel(
        backward_kernel,
        "backward",
        (shaped(helpers, channels, own_voxels, dtype=BF16), pltpu.HBM((3, rays), F32)),
        1,
        7,
        3,
        1,
        [
            pltpu.VMEM((640, 256), BF16),
            pltpu.VMEM((samples, rays), F32),
            pltpu.SMEM((samples, tiles), jnp.int32),
            pltpu.VMEM((3, rays), F32),
            pltpu.VMEM((brick_count, 256, 128), F32),
            pltpu.VMEM((8, rays), F32),
            pltpu.VMEM((samples // 4, 128, 256), F32),
            pltpu.VMEM((samples, rays), F32),
            pltpu.SemaphoreType.DMA((4,)),
        ],
        16,
        1 << 28,
    )(
        region,
        exchanged.reshape(regions * 4 * tiles, 128),
        rank,
        target,
        hats,
        planes,
        decoded,
        slopes,
        *far(mats, spacing, brick_ids),
    )
    received = lax.all_to_all(contribution, "helper", 0, 0)
    brick_grad = jnp.sum(received.astype(F32), axis=0)
    return colour, brick_grad


def solution(mesh):
    placed = (
        P(None, ("region", "helper")),
        P(None, "region", "helper"),
        P("region", "helper"),
        P("region", "helper"),
        P("helper", None),
        P(None, "helper"),
        P(),
        P(),
        P(),
        P(),
    )
    return jax.shard_map(
        per_device,
        mesh=mesh,
        in_specs=placed,
        out_specs=(P(None, "helper"), P(None, ("region", "helper"))),
        check_vma=False,
    )
```
